128 devices in a mesh: dp: 8 (over y, core), head: 16 (over z, x).
Axes of the slice: x: 4, y: 4, z: 4, core: 2. Of those that a mesh axis runs over, the one named last changes fastest.
Arguments:
- latent: bfloat16 [8192, 1536], P('dp', 'head'), may hold values from -6 to 6
- weight: bfloat16 [1536, 24576], P(None, 'head'), may hold values from -0.15625 to 0.15625
- query_grad: bfloat16 [8192, 24576], P('dp', 'head'), may hold values from -6 to 6
- master: float32 [1536, 24576], P('dp', 'head'), may hold values from -6 to 6
- first_moment: float32 [1536, 24576], P('dp', 'head'), may hold values from -6 to 6
- second_moment: float32 [1536, 24576], P('dp', 'head'), may hold values from 100 to 10000
Outputs:
- queries: bfloat16 [8192, 24576], P('dp', 'head')
- latent_grad: bfloat16 [8192, 1536], P('dp', 'head')
- new_master: float32 [1536, 24576], P('dp', 'head')
- new_first: float32 [1536, 24576], P('dp', 'head')
- new_second: float32 [1536, 24576], P('dp', 'head')
The draws below stay inside these ranges and needn't reach their ends.
All inputs are finite; a program needn't handle non-finite values.
Results may differ from the reference program's by a relative error of at most 0.014.
Values may be sent and summed in bfloat16 or wider, within the bound.
No kernel may reach another device: no remote copies, remote signals or barrier semaphores. Data moves between devices by JAX's collectives and lax.ppermute only.
A program may use at most 128 MiB of HBM per device.

```python
import math
import jax
import jax.numpy as jnp
from jax import lax

D = 1536
TOK_DEV = 1024
STEP = 10
QW = 24576
TOKENS = 8192
N_HEAD = 16


def raised(result, rng, source, target, shards_of, factor):
    def block_of(position):
        return (jnp.arange(result.shape[position]) // (result.shape[position] // shards_of)).reshape((-1,) + (1,) * (result.ndim - 1 - position))

    first = jax.random.permutation(rng, shards_of)[block_of(target)]
    other_side = (block_of(target) + shards_of // 2) % shards_of
    return jnp.where((block_of(source) == first) | (block_of(source) == other_side), factor * result, result)


def shard_levels(key, shape, split, least, largest):
    def one(dim, blocks):
        steps = jax.random.uniform(jax.random.fold_in(jax.random.fold_in(key, 6), dim), (blocks,), jnp.float32, least / len(split), largest / len(split))
        return jnp.repeat(jnp.exp(steps), shape[dim] // blocks).reshape((-1,) + (1,) * (len(shape) - dim - 1))

    level = one(*split[0])
    for cut in split[1:]:
        level = level * one(*cut)
    return level


def scatter_about(own_key, shape, spread, most, shards=(), kind=jnp.bfloat16):
    array = spread * jax.random.normal(own_key, shape, jnp.float32)
    if shards:
        array = array * shard_levels(own_key, shape, shards, -0.22, 0.18)
    return jnp.clip(array, -most, most).astype(kind)


def bell_draw_with(key, extent, scale, limit, pieces, heavy, kind=jnp.bfloat16):
    drawn = scale * jax.random.normal(key, extent, jnp.float32)
    if pieces:
        drawn = drawn * shard_levels(key, extent, pieces, -0.22, 0.18)
    return jnp.clip(raised(drawn, jax.random.fold_in(key, 3), *heavy), -limit, limit).astype(kind)


def setup_inputs(seed: int = 0) -> dict:
    seeds = jax.random.split(jax.random.key(seed), 7)
    latent = bell_draw_with(seeds[0], (TOKENS, D), 1.0, 6.0, ((0, 8), (1, 16)), (0, 1, 16, 2.0))
    weight = scatter_about(seeds[1], (D, QW), D ** -0.5, 0.15625, ((1, 16),))
    query_grad = scatter_about(seeds[2], (TOKENS, QW), 1.0, 6.0, ((0, 8), (1, 16)))
    master = scatter_about(seeds[3], (D, QW), 1.0, 6.0, ((0, 8), (1, 16)), jnp.float32)
    first_moment = scatter_about(seeds[4], (D, QW), 1.0, 6.0, ((0, 8), (1, 16)), jnp.float32)
    second_moment = jnp.clip(jnp.exp(math.log(10000.0) - 4.6051702 * jax.random.uniform(seeds[5], (D, QW), jnp.float32) ** shard_levels(seeds[5], (D, QW), ((0, 8), (1, 16)), -0.2, 0.2)), 100.0, 10000.0)
    return dict(latent=latent, weight=weight, query_grad=query_grad, master=master, first_moment=first_moment, second_moment=second_moment)


def reference(latent, weight, query_grad, master, first_moment, second_moment):
    queries = jnp.dot(latent, weight, preferred_element_type=jnp.float32).astype(jnp.bfloat16)
    width = QW // N_HEAD

    def add_heads(total, index):
        start = (index * width).astype(jnp.int32)
        grad_cols = lax.dynamic_slice_in_dim(query_grad, start, width, 1)
        weight_cols = lax.dynamic_slice_in_dim(weight, start, width, 1)
        part = lax.dot_general(grad_cols, weight_cols, (((1,), (1,)), ((), ())), preferred_element_type=jnp.float32)
        return (total + part.astype(jnp.bfloat16).astype(jnp.float32), None)
    lat_total, unused = lax.scan(add_heads, jnp.zeros((TOKENS, D), jnp.float32), jnp.arange(N_HEAD, dtype=jnp.int32))
    latent_grad = lat_total.astype(jnp.bfloat16)
    groups = TOKENS // TOK_DEV
    lat_groups = latent.reshape(groups, TOK_DEV, D)
    grad_groups = query_grad.reshape(groups, TOK_DEV, QW)

    def add_group(total, index):
        lat_one = lax.dynamic_index_in_dim(lat_groups, index, 0, keepdims=False)
        grad_one = lax.dynamic_index_in_dim(grad_groups, index, 0, keepdims=False)
        part = lax.dot_general(lat_one, grad_one, (((0,), (0,)), ((), ())), preferred_element_type=jnp.float32)
        return (total + part.astype(jnp.bfloat16).astype(jnp.float32), None)
    grad, unused = lax.scan(add_group, jnp.zeros((D, QW), jnp.float32), jnp.arange(groups, dtype=jnp.int32))
    new_first = 0.9 * first_moment + 0.1 * grad
    new_second = 0.95 * second_moment + 0.05 * grad * grad
    first_hat = new_first / (1.0 - 0.9 ** STEP)
    second_hat = new_second / (1.0 - 0.95 ** STEP)
    new_master = master - 0.01 * (first_hat / (jnp.sqrt(second_hat) + 1e-08) + 0.1 * master)
    return (queries, latent_grad, new_master, new_first, new_second)
```

```python
import jax
import jax.numpy as jnp
import numpy as np
from jax import lax
from jax.experimental import pallas as pl
from jax.experimental.pallas import tpu as pltpu
from jax.sharding import PartitionSpec as P

STEP = 10
BOTH = ("dp", "head")
B = 96
F32 = jnp.float32
BF16 = jnp.bfloat16
MIB = 1024 * 1024


def device(y, c, z, x):
    return ((y % 4) * 2 + c % 2) * 16 + (z % 4) * 4 + x % 4


def moved(step):
    return [
        (device(y, c, z, x), device(*step(y, c, z, x)))
        for y in range(4)
        for c in range(2)
        for z in range(4)
        for x in range(4)
    ]


def along_a(d):
    return moved(lambda y, c, z, x: (y, c, z, x + d) if c else (y, c, z + d, x))


def along_b(d):
    return moved(lambda y, c, z, x: (y, c, z + d, x) if c else (y, c, z, x + d))


def along_y(d):
    return moved(lambda y, c, z, x: (y + d, c, z, x))


PARTNER = moved(lambda y, c, z, x: (y, 1 - c, z, x))


def sent(x, pairs):
    return lax.ppermute(x, BOTH, pairs)


def indices():
    rows = []
    for dp in range(8):
        for head in range(16):
            y, c, z, x = dp // 2, dp % 2, head // 4, head % 4
            a, b = (x, z) if c else (z, x)

            def at(i, j):
                i, j = i % 4, j % 4
                return 4 * j + i if c else 4 * i + j

            to = [at(a + i, b + j) for i in range(4) for j in range(4)]
            come = [at(a - i, b - j) for i in range(4) for j in range(4)]
            picks = []
            for d in range(4):
                mine = []
                other = []
                for j in (0, 1):
                    u, v = (z - y - d) % 4, (x - 2 * c - j) % 4
                    mine += [v, u] if c else [u, v]
                    other += [u, v] if c else [v, u]
                picks += mine + other
            rows.append(to + come + picks)
    return np.array(rows, np.int32)


TABLE = indices()


def lat_grad_kernel(idx, w0, w1, w2, w3, g, *outs):
    w = jnp.concatenate([w0[...], w1[...], w2[...], w3[...]], axis=0)
    r = lax.dot_general(w, g[...], (((1,), (1,)), ((), ())), preferred_element_type=F32)
    for k, out in enumerate(outs):

        @pl.when(pl.program_id(0) == k)
        def _():
            out[...] = r.astype(BF16)


def lat_grad_parts(weight, query_grad, heads):
    return pl.pallas_call(
        lat_grad_kernel,
        grid_spec=pltpu.PrefetchScalarGridSpec(
            num_scalar_prefetch=1,
            grid=(2,),
            in_specs=[pl.BlockSpec((B, 1536), lambda d, idx, j=j: (idx[d * 4 + j], 0)) for j in range(4)]
            + [pl.BlockSpec((1024, 1536), lambda d, idx: (0, 0))],
            out_specs=[pl.BlockSpec((4 * B, 1024), lambda d, idx: (0, 0))] * 2,
        ),
        out_shape=[jax.ShapeDtypeStruct((4 * B, 1024), BF16)] * 2,
        compiler_params=pltpu.CompilerParams(vmem_limit_bytes=24 * MIB),
        cost_estimate=pl.CostEstimate(flops=1024 * 1536 * 1536, bytes_accessed=6000000, transcendentals=0),
    )(heads, weight, weight, weight, weight, query_grad)


def assemble_kernel(idx, s0, s1, s2, s3, full):
    for k2, src in enumerate((s0, s1, s2, s3)):
        for k1 in range(4):
            full[idx[k2 * 4 + k1]] = src[k1]


def assembled(pieces, idx):
    return pl.pallas_call(
        assemble_kernel,
        grid_spec=pltpu.PrefetchScalarGridSpec(
            num_scalar_prefetch=1,
            grid=(),
            in_specs=[pl.BlockSpec(memory_space=pltpu.VMEM)] * 4,
            out_specs=pl.BlockSpec(memory_space=pltpu.VMEM),
        ),
        out_shape=jax.ShapeDtypeStruct((16, B, 1024), BF16),
        compiler_params=pltpu.CompilerParams(vmem_limit_bytes=8 * MIB),
        cost_estimate=pl.CostEstimate(flops=0, bytes_accessed=6000000, transcendentals=0),
        name="assemble",
    )(idx, *pieces)


def w_grad_kernel(idx, *refs):
    pieces = (refs[:4], refs[4:8])
    q, q_other, out0, out1, lhs = refs[8:]

    @pl.when(pl.program_id(0) == 0)
    def _():
        for side in range(2):
            for j in range(4):
                at = (j // 2) * 8 + side * 4 + (j % 2) * 2
                for k2 in range(4):

                    @pl.when(idx[at] == k2)
                    def _():
                        lhs[side, j * B : (j + 1) * B] = pieces[side][k2][idx[at + 1]]

    r = jnp.dot(lhs[0], q[...], preferred_element_type=F32)
    r += jnp.dot(lhs[1], q_other[...], preferred_element_type=F32)
    r = r.astype(BF16)
    out0[...] = r[:192]
    out1[...] = r[192:]


def w_grad_parts(own, other, g, g_other, picks):
    n = 3
    return pl.pallas_call(
        w_grad_kernel,
        grid_spec=pltpu.PrefetchScalarGridSpec(
            num_scalar_prefetch=1,
            grid=(n,),
            in_specs=[pl.BlockSpec(memory_space=pltpu.VMEM)] * 8
            + [pl.BlockSpec((1024, 1536 // n), lambda t, idx: (0, t))] * 2,
            out_specs=[pl.BlockSpec((192, 1536 // n), lambda t, idx: (0, t))] * 2,
            scratch_shapes=[pltpu.VMEM((2, 384, 1024), BF16)],
        ),
        out_shape=[jax.ShapeDtypeStruct((192, 1536), BF16)] * 2,
        compiler_params=pltpu.CompilerParams(vmem_limit_bytes=24 * MIB),
        cost_estimate=pl.CostEstimate(flops=2 * 384 * 2048 * 1536, bytes_accessed=9000000, transcendentals=0),
    )(picks, *own, *other, g, g_other)


def update(grad, master, first_moment, second_moment):
    new_first = 0.9 * first_moment + 0.1 * grad
    new_second = 0.95 * second_moment + 0.05 * grad * grad
    first_hat = new_first / (1.0 - 0.9**STEP)
    second_hat = new_second / (1.0 - 0.95**STEP)
    new_master = master - 0.01 * (first_hat / (jnp.sqrt(second_hat) + 1e-08) + 0.1 * master)
    return new_master, new_first, new_second


def sends(blocks, pairs, steps=(1, 2, 3)):
    out = {}
    for d in steps:
        out[d] = sent(blocks(d), pairs(d))
    return out


def pick(table, *spans):
    return jnp.concatenate([table[i:j] for i, j in spans])


def on_device(latent, weight, query_grad, master, first_moment, second_moment):
    table = lax.dynamic_slice(jnp.asarray(TABLE), (lax.axis_index("dp") * 16 + lax.axis_index("head"), 0), (1, 64))[0]

    own = latent.T
    near = sends(lambda d: own, along_b)
    g_other = sent(query_grad, PARTNER)
    row = jnp.stack([own, near[1], near[2], near[3]])
    rows = {0: row, **sends(lambda d: row, along_a)}
    parts = {}
    parts[1], parts[3] = lat_grad_parts(weight, query_grad, pick(table, (4, 8), (12, 16)))
    parts[2], parts[0] = lat_grad_parts(weight, query_grad, pick(table, (8, 12), (0, 4)))
    got = sends(lambda d: parts[d], along_a)
    others = sends(lambda d: rows[d], lambda d: PARTNER, (0, 1, 3, 2))

    mine = [rows[d] for d in range(4)]
    theirs = [others[d] for d in range(4)]
    sums = {}
    sums[1], sums[3] = w_grad_parts(mine, theirs, query_grad, g_other, pick(table, (40, 48), (56, 64)))
    sums[2], sums[0] = w_grad_parts(mine, theirs, query_grad, g_other, pick(table, (48, 56), (32, 40)))
    come = sends(lambda d: sums[d], along_y)

    half = (parts[0].astype(F32) + got[1].astype(F32)) + (got[2].astype(F32) + got[3].astype(F32))
    half = half.astype(BF16).reshape(4, B, 1024)
    final = sends(lambda d: half[d], along_b)

    full = assembled(mine, table[16:32]).reshape(1536, 1024)
    queries = lax.dot_general(full, weight, (((0,), (0,)), ((), ())), preferred_element_type=F32).astype(BF16)
    latent_grad = sum(p.astype(F32) for p in (half[0], final[1], final[2], final[3])).astype(BF16).T
    grad = sum(s.astype(F32) for s in (sums[0], come[1], come[2], come[3]))
    return (queries, latent_grad, *update(grad, master, first_moment, second_moment))


def solution(mesh):
    spec = P("dp", "head")
    return jax.shard_map(
        on_device,
        mesh=mesh,
        in_specs=(spec, P(None, "head"), spec, spec, spec, spec),
        out_specs=(spec,) * 5,
        check_vma=False,
    )
```
